32 devices in a mesh: band: 4 (over y, x), ga: 8 (over z, core).
Axes of the slice: x: 2, y: 2, z: 4, core: 2. Of those that a mesh axis runs over, the one named last changes fastest.
Arguments:
- psi: float32 [4096, 4096], P('band', 'ga'), may hold values from -6 to 6
- lower: float32 [4096, 4096], P('band', 'ga'), as said below
Outputs:
- orthonormal: float32 [4096, 4096], P('band', 'ga')
- block_intersection: float32 [4096, 1024], P('band')
The draws below stay inside these ranges and needn't reach their ends.
Inputs may be any that keep to these rules, and one draw needn't show every extreme that they name: lower is lower triangular with its diagonal between 1 and 2.
All inputs are finite; a program needn't handle non-finite values.
Results may differ from the reference program's by a relative error of at most 0.00022.
Values sent between devices are 32-bit elements; how exact they have to be, the bound alone decides.
A program may use at most 64 MiB of HBM per device.

```python
import math
import jax
import jax.numpy as jnp
from jax import lax

NB = 4096
NG = 4096
N_BAND = 4


def draw_lower(key, part):
    first, second = jax.random.split(jax.random.fold_in(key, 11))
    spread = jax.random.normal(first, (NB, NB), jnp.float32) * (2.0 / math.sqrt(NB))
    middle = jax.random.uniform(second, (NB,), jnp.float32, 1.0, 2.0)
    rowpos = lax.broadcasted_iota(jnp.int32, (NB, NB), 0)
    colpos = lax.broadcasted_iota(jnp.int32, (NB, NB), 1)
    return jnp.where(rowpos > colpos, spread, 0.0) + jnp.diag(middle)


def shard_levels(stream_key, extent, pieces, smallest, largest):
    def one(dim, shards_of):
        heights = jax.random.uniform(jax.random.fold_in(jax.random.fold_in(stream_key, 6), dim), (shards_of,), jnp.float32, smallest / len(pieces), largest / len(pieces))
        return jnp.repeat(jnp.exp(heights), extent[dim] // shards_of).reshape((-1,) + (1,) * (len(extent) - dim - 1))

    level = one(*pieces[0])
    for cut in pieces[1:]:
        level = level * one(*cut)
    return level


def bell_draw(key, extent, deviation, bound, shards=(), kind=jnp.bfloat16):
    array = deviation * jax.random.normal(key, extent, jnp.float32)
    if shards:
        array = array * shard_levels(key, extent, shards, -0.22, 0.18)
    return jnp.clip(array, -bound, bound).astype(kind)


def setup_inputs(seed: int = 0) -> dict:
    splits = jax.random.split(jax.random.key(seed), 3)
    psi = bell_draw(splits[0], (NB, NG), 1.0, 6.0, ((0, 4), (1, 8)), jnp.float32)
    lower = draw_lower(jax.random.fold_in(splits[2], 71), 0)
    return {"psi": psi, "lower": lower}


def reference(psi, lower):
    solved = jax.scipy.linalg.solve_triangular(lower, psi, lower=True)
    blocks = solved.reshape(N_BAND, NB // N_BAND, NG)
    intersection = jnp.einsum('bik,bjk->bij', blocks, blocks, precision=lax.Precision.HIGHEST) / NG
    return (solved, intersection.reshape(NB, NB // N_BAND))
```

```python
import jax
import jax.numpy as jnp
from jax import lax
from jax.sharding import PartitionSpec as P

BASE = 128
PIECES = 2


def mm(a, b, precision):
    return jnp.matmul(a, b, precision=precision, preferred_element_type=jnp.float32)


def tri_inverse(tile):
    n = tile.shape[0]
    base = min(BASE, n)
    best = lax.Precision.HIGHEST
    blocks = jnp.stack([tile[i : i + base, i : i + base] for i in range(0, n, base)])
    row = lax.broadcasted_iota(jnp.int32, (base, base), 0)
    col = lax.broadcasted_iota(jnp.int32, (base, base), 1)
    inverse = jnp.where(row == col, 1.0 / jnp.where(row == col, blocks, 1.0), 0.0)
    size = 1
    while size < base:
        off = (row // (2 * size) == col // (2 * size)) & (row // size > col // size)
        below = jnp.where(off, blocks, 0.0)
        inverse = inverse - mm(inverse, mm(below, inverse, best), best)
        size *= 2
    while size < n:
        below = jnp.stack(
            [tile[i + size : i + 2 * size, i : i + size] for i in range(0, n, 2 * size)]
        )
        first, second = inverse[0::2], inverse[1::2]
        corner = -mm(second, mm(below, first, best), best)
        top = jnp.concatenate([first, jnp.zeros_like(first)], axis=2)
        bottom = jnp.concatenate([corner, second], axis=2)
        inverse = jnp.concatenate([top, bottom], axis=1)
        size *= 2
    return inverse[0]


def local(psi, lower):
    high = lax.Precision.HIGH
    myblock = lax.axis_index("band")
    sections = lax.axis_size("band")
    nrows, width = psi.shape
    full_rows = lax.all_gather(lower, "ga", axis=1, tiled=True)
    own_tile = lax.dynamic_slice_in_dim(full_rows, myblock * nrows, nrows, 1)
    inverse = tri_inverse(own_tile)
    span = width // PIECES
    rest = [psi[:, i * span : (i + 1) * span] for i in range(PIECES)]
    for s in range(sections - 1):
        tile = full_rows[:, s * nrows : (s + 1) * nrows]
        for i in range(PIECES):
            ready = mm(inverse, rest[i], high)
            arrived = lax.ppermute(ready, "band", [(s, s + 1)])
            for t in range(s + 2, sections):
                arrived = arrived + lax.ppermute(ready, "band", [(s, t)])
            rest[i] = rest[i] - mm(tile, arrived, high)
    solved = jnp.concatenate([mm(inverse, rest[i], high) for i in range(PIECES)], axis=1)
    mine = lax.dot_general(
        solved, solved, (((1,), (1,)), ((), ())), precision=high, preferred_element_type=jnp.float32
    )
    intersection = lax.psum(mine, "ga") / (width * lax.axis_size("ga"))
    return (solved, intersection)


def solution(mesh):
    return jax.shard_map(
        local,
        mesh=mesh,
        in_specs=(P("band", "ga"), P("band", "ga")),
        out_specs=(P("band", "ga"), P("band", None)),
        check_vma=False,
    )
```
